32 devices in a mesh: dp: 8 (over z, y), group: 4 (over x, core).
Axes of the slice: x: 2, y: 2, z: 4, core: 2. Of those that a mesh axis runs over, the one named last changes fastest.
Arguments:
- images: bfloat16 [32, 729, 1152], P(('dp', 'group')), may hold values from -6 to 6
- cotangent: bfloat16 [32, 729, 1152], P(('dp', 'group')), may hold values from -6 to 6
- flags: int32 [32], P(('dp', 'group')), may hold values 0 or 1
- master: float32 [15261696], P(('dp', 'group')), may hold values from -1.2 to 1.4, as said below
- first_moment: float32 [15261696], P(('dp', 'group')), may hold values from -6 to 6
- second_moment: float32 [15261696], P(('dp', 'group')), may hold values from 1 to 100
Outputs:
- layer_out: bfloat16 [32, 729, 1152], P(('dp', 'group'))
- input_grad: bfloat16 [32, 729, 1152], P(('dp', 'group'))
- weight_grad: float32 [15261696], P(('dp', 'group'))
- new_master: float32 [15261696], P(('dp', 'group'))
- new_first: float32 [15261696], P(('dp', 'group'))
- new_second: float32 [15261696], P(('dp', 'group'))
The draws below stay inside these ranges and needn't reach their ends.
Inputs may be any that keep to these rules, and one draw needn't show every extreme that they name: `master`: parameters of order one: gains near 1, biases, and weights scaled by their fan-in.
All inputs are finite; a program needn't handle non-finite values. No bound on the sum of `flags` on one device may be relied on, other than what follows from the above.
Results may differ from the reference program's by a relative error of at most 0.0087.
Values may be sent and summed in bfloat16 or wider, within the bound.
No kernel may reach another device: no remote copies, remote signals or barrier semaphores. Data moves between devices by JAX's collectives and lax.ppermute only.
A program may use at most 256 MiB of HBM per device.

```python
import math
import jax
import jax.numpy as jnp
from jax import lax

D = 1152
HEADS = 16
FF = 4304
SEQ = 729
HEAD_DIM = 72
IMAGES = 32
SLICE_LEN = 3814772
SHARD = 476928
FLAT = 15261696
N_DP = 8
N_GROUP = 4


def slice_scales(group_index):
    part_width = D // N_GROUP
    part_hidden = FF // N_GROUP
    entries = [(D * 3 * part_width, D ** (-0.5), 0.0), (2 * part_width, 0.3, 0.0), (part_width * D, 3.0 * D ** (-0.5), 0.0), (D * part_hidden, D ** (-0.5), 0.0), (part_hidden, 0.3, 0.0), (part_hidden * D, FF ** (-0.5), 0.0)]
    if group_index == 0:
        entries = entries + [(D, 0.1, 1.0), (D, 0.3, 0.0), (D, 0.3, 0.0), (D, 0.1, 1.0), (D, 0.3, 0.0), (D, 0.3, 0.0)]
    else:
        entries = entries + [(6 * D, 0.02, 0.0)]
    entries = entries + [(N_DP * SHARD - SLICE_LEN, 0.02, 0.0)]
    return entries


def draw_master(key, part):
    scale_rows = []
    center_rows = []
    for group_index in range(N_GROUP):
        entries = slice_scales(group_index)
        scale_rows.append(jnp.concatenate([jnp.full((count,), spread, jnp.float32) for count, spread, center in entries]))
        center_rows.append(jnp.concatenate([jnp.full((count,), center, jnp.float32) for count, spread, center in entries]))
    scale_vec = jnp.stack(scale_rows).reshape(N_GROUP, N_DP, SHARD).transpose(1, 0, 2).reshape(FLAT)
    center_vec = jnp.stack(center_rows).reshape(N_GROUP, N_DP, SHARD).transpose(1, 0, 2).reshape(FLAT)
    noise_vec = jax.random.truncated_normal(key, -4.0, 4.0, (FLAT,), jnp.float32)
    return center_vec + scale_vec * noise_vec


def touch_ends(drawn, stream_key, low, top_value):
    place = [jax.random.randint(jax.random.fold_in(stream_key, axis), (), 0, length) for axis, length in enumerate(drawn.shape)]
    longest = drawn.shape.index(max(drawn.shape))
    neighbour = place[:longest] + [(place[longest] + 1) % drawn.shape[longest]] + place[longest + 1:]
    return drawn.at[tuple(place)].set(low).at[tuple(neighbour)].set(top_value)


def steps_of(key, shape, split, low, top_value):
    factor_of, own = 1.0, jax.random.fold_in(key, 6)
    for dim, parts in split:
        heights = jnp.exp(jax.random.uniform(jax.random.fold_in(own, dim), (parts,), jnp.float32, low / len(split), top_value / len(split)))
        factor_of = factor_of * jnp.repeat(heights, shape[dim] // parts).reshape([-1 if axis == dim else 1 for axis in range(len(shape))])
    return factor_of


def normal_values(key, shape, scale, most, split=(), kind=jnp.bfloat16):
    result = jax.random.normal(key, shape, jnp.float32) * scale
    if len(split) > 0:
        result = steps_of(key, shape, split, -0.22, 0.18) * result
    return jnp.clip(result, min=-most, max=most).astype(kind)


def setup_inputs(seed: int = 0) -> dict:
    key_list = jax.random.split(jax.random.key(seed), 7)
    images = normal_values(key_list[0], (IMAGES, SEQ, D), 1.0, 6.0, ((0, 32),))
    cotangent = normal_values(key_list[1], (IMAGES, SEQ, D), 1.0, 6.0, ((0, 32),))
    flags = touch_ends((jax.random.randint(key_list[2], (IMAGES,), 0, 256) < 89).astype(jnp.int32), jax.random.fold_in(key_list[2], 1), 0, 1)
    master = draw_master(jax.random.fold_in(key_list[6], 71), 0)
    first_moment = normal_values(key_list[4], (FLAT,), 1.0, 6.0, ((0, 32),), jnp.float32)
    second_moment = jnp.clip(jnp.exp(math.log(100.0) - 4.6051702 * jax.random.uniform(key_list[5], (FLAT,), jnp.float32) ** steps_of(key_list[5], (FLAT,), ((0, 32),), -0.2, 0.2)), 1.0, 100.0)
    return {"images": images, "cotangent": cotangent, "flags": flags, "master": master, "first_moment": first_moment, "second_moment": second_moment}


@jax.custom_vjp
def low(v):
    return lax.optimization_barrier(v.astype(jnp.bfloat16)).astype(jnp.float32)

@jax.custom_vjp
def low_back(v):
    return v

def low_keep(v):
    return (low(v), None)

def low_pass(kept, grad):
    return (grad,)

def back_keep(v):
    return (v, None)

def back_low(kept, grad):
    return (low(grad),)
low.defvjp(low_keep, low_pass)
low_back.defvjp(back_keep, back_low)
norm_eps = 1e-06
learn_rate = 0.01
beta_one = 0.9
beta_two = 0.999
adam_eps = 1e-08
adam_step = 10

def slice_shapes():
    part_width = D // N_GROUP
    part_hidden = FF // N_GROUP
    return [(D, 3, part_width), (2, part_width), (part_width, D), (D, part_hidden), (part_hidden,), (part_hidden, D)]

def assemble(flat_vec):
    regions = flat_vec.reshape(N_DP, N_GROUP, SHARD).transpose(1, 0, 2).reshape(N_GROUP, N_DP * SHARD)
    stacks = []
    offset = 0
    for dims_tuple in slice_shapes():
        length = 1
        for extent in dims_tuple:
            length = length * extent
        stacks.append(regions[:, offset:offset + length].reshape((N_GROUP,) + dims_tuple))
        offset = offset + length
    shared = regions[0, offset:offset + 6 * D].reshape(6, D)
    qkv_st, qv_st, out_st, up_st, upb_st, down_st = stacks
    w_qkv = qkv_st.transpose(1, 2, 0, 3).reshape(D, 3 * D)
    qv_bias = qv_st.transpose(1, 0, 2).reshape(2 * D)
    w_out = out_st.reshape(D, D)
    w_up = up_st.transpose(1, 0, 2).reshape(D, FF)
    up_bias = upb_st.reshape(FF)
    w_down = down_st.reshape(FF, D)
    return [shared[0], shared[1], w_qkv, qv_bias, w_out, shared[2], shared[3], shared[4], w_up, up_bias, w_down, shared[5]]

def disassemble(grads):
    g_gain_one, g_bias_one, g_qkv, g_qv, g_out, g_out_bias, g_gain_two, g_bias_two, g_up, g_up_bias, g_down, g_down_bias = grads
    part_width = D // N_GROUP
    part_hidden = FF // N_GROUP
    qkv_st = g_qkv.reshape(D, 3, N_GROUP, part_width).transpose(2, 0, 1, 3)
    qv_st = g_qv.reshape(2, N_GROUP, part_width).transpose(1, 0, 2)
    out_st = g_out.reshape(N_GROUP, part_width, D)
    up_st = g_up.reshape(D, N_GROUP, part_hidden).transpose(1, 0, 2)
    upb_st = g_up_bias.reshape(N_GROUP, part_hidden)
    down_st = g_down.reshape(N_GROUP, part_hidden, D)
    shared = jnp.concatenate([g_gain_one, g_bias_one, g_out_bias, g_gain_two, g_bias_two, g_down_bias])
    tails = jnp.concatenate([shared[None], jnp.zeros((N_GROUP - 1, 6 * D), jnp.float32)], 0)
    pieces = [item_s.reshape(N_GROUP, -1) for item_s in [qkv_st, qv_st, out_st, up_st, upb_st, down_st]]
    region = jnp.concatenate(pieces + [tails, jnp.zeros((N_GROUP, N_DP * SHARD - SLICE_LEN), jnp.float32)], 1)
    return region.reshape(N_GROUP, N_DP, SHARD).transpose(1, 0, 2).reshape(FLAT)

def highest(left_mat, right_mat):
    return jnp.dot(left_mat, right_mat, precision=lax.Precision.HIGHEST)

def layer_norm(values, gain_vec, bias_vec):
    center = values - lax.optimization_barrier(jnp.mean(values, -1, keepdims=True))
    variance = lax.optimization_barrier(jnp.mean(center * center, -1, keepdims=True))
    return center * lax.rsqrt(variance + norm_eps) * gain_vec + bias_vec

def forward(param_list, tokens, flag_val):
    gain_one, bias_one, w_qkv, qv_bias, w_out, out_bias, gain_two, bias_two, w_up, up_bias, w_down, down_bias = [low(item_p) for item_p in param_list]
    seq_len = tokens.shape[0]
    normed = low(layer_norm(tokens, gain_one, bias_one))
    bias_full = jnp.concatenate([qv_bias[:D], jnp.zeros((D,), jnp.float32), qv_bias[D:]])
    joined = low(low_back(highest(normed, w_qkv) + bias_full))
    queries = joined[:, :D].reshape(seq_len, HEADS, HEAD_DIM)
    key_rows = joined[:, D:2 * D].reshape(seq_len, HEADS, HEAD_DIM)
    value_rows = joined[:, 2 * D:].reshape(seq_len, HEADS, HEAD_DIM)
    raw_scores = low_back(jnp.einsum('qhd,khd->hqk', queries, key_rows, precision=lax.Precision.HIGHEST))
    attn_probs = jax.nn.softmax(raw_scores * HEAD_DIM ** (-0.5), axis=-1)
    mixed = jnp.einsum('hqk,khd->qhd', low(attn_probs), value_rows, precision=lax.Precision.HIGHEST)
    mixed = low(low_back(mixed.reshape(seq_len, D)))
    hidden_state = tokens + low_back(highest(mixed, w_out) + out_bias)
    normed_two = low(layer_norm(hidden_state, gain_two, bias_two))
    pre_act = low_back(highest(normed_two, w_up) + up_bias)
    activ = low(jax.nn.gelu(pre_act, approximate=True))
    branch = low_back(highest(activ, w_down) + down_bias)
    return flag_val * (hidden_state + branch)

def reference(images, cotangent, flags, master, first_moment, second_moment):
    params = assemble(master)

    def one_image(totals, inputs):
        tokens, cot_rows, flag_int = inputs
        flag_val = flag_int.astype(jnp.float32)
        output, pullback = jax.vjp(lambda param_list, token_rows: forward(param_list, token_rows, flag_val), params, tokens.astype(jnp.float32))
        grads_list, token_grad = pullback(cot_rows.astype(jnp.float32))
        totals = [total_v + grad_v for total_v, grad_v in zip(totals, grads_list)]
        return (totals, (output.astype(jnp.bfloat16), token_grad.astype(jnp.bfloat16)))
    initial = [jnp.zeros_like(item_p) for item_p in params]
    totals, (outputs, input_grads) = lax.scan(one_image, initial, (images, cotangent, flags))
    weight_grad = disassemble(totals)
    new_first = beta_one * first_moment + (1.0 - beta_one) * weight_grad
    new_second = beta_two * second_moment + (1.0 - beta_two) * weight_grad * weight_grad
    corrected = new_first / (1.0 - beta_one ** adam_step)
    var_hat = new_second / (1.0 - beta_two ** adam_step)
    new_master = master - learn_rate * corrected / (jnp.sqrt(var_hat) + adam_eps)
    return (outputs, input_grads, weight_grad, new_master, new_first, new_second)
```

```python
import math

import jax
import jax.numpy as jnp
from jax import lax
from jax.experimental import pallas as pl
from jax.experimental.pallas import tpu as pltpu
from jax.sharding import PartitionSpec as P

D = 1152
HEADS = 16
FF = 4304
HEAD_DIM = D // HEADS
LANES = 128
BLOCK = 32
MARGIN = 320
SPAN = 1152

norm_eps = 1e-06
learn_rate = 0.01
beta_one = 0.9
beta_two = 0.999
adam_eps = 1e-08
adam_step = 10

f32 = jnp.float32
bf16 = jnp.bfloat16
BOTH = ("dp", "group")


def region_items(group_count):
    part_width = D // group_count
    part_hidden = FF // group_count
    shapes = [
        ("qkv", D, 3 * part_width),
        ("qv", 1, 2 * part_width),
        ("out", part_width, D),
        ("up", D, part_hidden),
        ("upb", 1, part_hidden),
        ("down", part_hidden, D),
        ("tail", 1, 6 * D),
    ]
    items = {}
    offset = 0
    for name, rows, width in shapes:
        items[name] = (offset, rows, width)
        offset = offset + rows * width
    return items


def phase_count(width):
    return LANES // math.gcd(width, LANES)


def lane_rows(start, length):
    first = start // LANES
    lane = start % LANES
    return first, lane, -(-(lane + length) // LANES)


def round_up(value, step):
    return -(-value // step) * step


def vector_rows(items):
    places = {}
    at = 0
    for name in ("qv", "upb", "tail"):
        start, _, length = items[name]
        first, lane, count = lane_rows(start, length)
        places[name] = (at, first, lane, count, length)
        at = at + round_up(count, 8)
    return places, at


def unpack_regions(pieces, group_count):
    piece_count, regions, shard_rows, _ = pieces.shape
    items = region_items(group_count)
    places, vec_rows = vector_rows(items)
    region_rows = piece_count * shard_rows
    part_width = D // group_count
    qkv_tiles = -(-3 * part_width // LANES)
    up_start, up_rows, up_width = items["up"]
    up_phases = phase_count(up_width)
    up_stride = up_width * up_phases // LANES
    up_units = up_rows // up_phases
    qkv_start, qkv_rows, qkv_width = items["qkv"]
    qkv_phases = phase_count(qkv_width)
    qkv_stride = qkv_width * qkv_phases // LANES
    wide_tiles = SPAN // LANES
    out_pad = round_up(part_width, LANES)

    def kernel(in_ref, qkv_ref, out_ref, up_ref, down_ref, vec_ref, flat, tmp, tall):
        chunk = 64
        whole = shard_rows // chunk
        for piece in range(piece_count):

            def widen(step, carry, piece=piece):
                rows = pl.ds(pl.multiple_of(step * chunk, chunk), chunk)
                flat[pl.ds(step * chunk + piece * shard_rows, chunk), :] = in_ref[piece, 0, rows, :].astype(f32)
                return carry

            lax.fori_loop(0, whole, widen, 0)
            left = shard_rows - whole * chunk
            if left:
                flat[pl.ds(piece * shard_rows + whole * chunk, left), :] = in_ref[
                    piece, 0, pl.ds(whole * chunk, left), :
                ].astype(f32)

        def shifted(first, second, lane_at, rows):
            if lane_at == 0:
                return first
            lane = lax.broadcasted_iota(jnp.int32, (rows, LANES), 1)
            return pltpu.roll(jnp.where(lane >= lane_at, first, second), LANES - lane_at, 1)

        units = BLOCK // qkv_phases

        def qkv_step(step, carry):
            for phase in range(qkv_phases):
                first, lane_at, _ = lane_rows(qkv_start + phase * qkv_width, 1)
                loads = [
                    flat[pl.ds(first + tile + qkv_stride * units * step, units, stride=qkv_stride), :]
                    for tile in range(qkv_tiles + 1)
                ]
                for tile in range(qkv_tiles):
                    value = shifted(loads[tile], loads[tile + 1], lane_at, units)
                    valid = qkv_width - tile * LANES
                    if valid < LANES:
                        lane = lax.broadcasted_iota(jnp.int32, (units, LANES), 1)
                        value = jnp.where(lane < valid, value, 0.0)
                    tmp[tile, pl.ds(phase, units, stride=qkv_phases), :] = value
            rows = pl.ds(pl.multiple_of(step * BLOCK, BLOCK), BLOCK)
            for tile in range(qkv_tiles):
                qkv_ref[rows, tile * LANES : (tile + 1) * LANES] = tmp[tile].astype(bf16)
            return carry

        lax.fori_loop(0, qkv_rows // BLOCK, qkv_step, 0)

        def straight(name, target):
            start, rows_total, width = items[name]
            tiles = width // LANES
            first, lane_at, _ = lane_rows(start, 1)
            blocks = -(-rows_total // BLOCK)

            def step_of(step, carry):
                loads = [
                    flat[pl.ds(first + tile + tiles * BLOCK * step, BLOCK, stride=tiles), :]
                    for tile in range(tiles + 1)
                ]
                row = lax.broadcasted_iota(jnp.int32, (BLOCK, LANES), 0) + step * BLOCK
                rows = pl.ds(pl.multiple_of(step * BLOCK, BLOCK), BLOCK)
                for tile in range(tiles):
                    value = shifted(loads[tile], loads[tile + 1], lane_at, BLOCK)
                    if rows_total % BLOCK:
                        value = jnp.where(row < rows_total, value, 0.0)
                    target[rows, tile * LANES : (tile + 1) * LANES] = value.astype(bf16)
                return carry

            lax.fori_loop(0, blocks, step_of, 0)
            rest = target.shape[0] - blocks * BLOCK
            if rest:
                target[pl.ds(blocks * BLOCK, rest), :] = jnp.zeros((rest, width), bf16)

        straight("out", out_ref)
        straight("down", down_ref)

        def up_step(tile, carry):
            lane = lax.broadcasted_iota(jnp.int32, (up_units, LANES), 1)
            for phase in range(up_phases):
                first, lane_at, _ = lane_rows(up_start + phase * up_width, 1)
                one = flat[pl.ds(first + tile, up_units, stride=up_stride), :]
                two = flat[pl.ds(first + tile + 1, up_units, stride=up_stride), :]
                value = shifted(one, two, lane_at, up_units)
                value = jnp.where(lane < up_width - tile * LANES, value, 0.0)
                tall[pl.ds(phase, up_units, stride=up_phases), :] = value
            up_ref[:, pl.ds(pl.multiple_of(tile * LANES, LANES), LANES)] = tall[...].astype(bf16)
            return carry

        lax.fori_loop(0, wide_tiles, up_step, 0)
        for name in places:
            at, first, _, count, _ = places[name]
            take = round_up(count, 8)
            vec_ref[0, pl.ds(at, take), :] = flat[pl.ds(first, take), :]

    return pl.pallas_call(
        kernel,
        grid=(regions,),
        in_specs=[pl.BlockSpec((piece_count, 1, shard_rows, LANES), lambda r: (0, r, 0, 0))],
        out_specs=[
            pl.BlockSpec((D, qkv_tiles * LANES), lambda r: (0, r)),
            pl.BlockSpec((out_pad, D), lambda r: (r, 0)),
            pl.BlockSpec((D, SPAN), lambda r: (0, r)),
            pl.BlockSpec((SPAN, D), lambda r: (r, 0)),
            pl.BlockSpec((1, vec_rows, LANES), lambda r: (r, 0, 0)),
        ],
        out_shape=[
            jax.ShapeDtypeStruct((D, regions * qkv_tiles * LANES), bf16),
            jax.ShapeDtypeStruct((regions * out_pad, D), bf16),
            jax.ShapeDtypeStruct((D, regions * SPAN), bf16),
            jax.ShapeDtypeStruct((regions * SPAN, D), bf16),
            jax.ShapeDtypeStruct((regions, vec_rows, LANES), f32),
        ],
        scratch_shapes=[
            pltpu.VMEM((region_rows + MARGIN, LANES), f32),
            pltpu.VMEM((qkv_tiles, BLOCK, LANES), f32),
            pltpu.VMEM((D, LANES), f32),
        ],
        compiler_params=pltpu.CompilerParams(vmem_limit_bytes=60 * 1024 * 1024),
        name="unpack_regions",
    )(pieces)


def pack_range(grads, vectors, low_row, high_row, group_count, place=None):
    items = region_items(group_count)
    part_width = D // group_count
    total = high_row - low_row
    base = MARGIN - low_row
    work = []
    for name in ("qkv", "out", "up", "down"):
        start, rows, width = items[name]
        begin = max(0, (low_row * LANES - start) // width)
        stop = min(rows, -(-(high_row * LANES - start) // width))
        if stop > begin:
            begin = begin // BLOCK * BLOCK
            work.append((name, begin, min(round_up(stop, BLOCK), rows) - begin))
    vec_work = []
    for name in ("qv", "upb"):
        start, _, length = items[name]
        first, lane, count = lane_rows(start, length)
        if first < high_row and first + count > low_row:
            vec_work.append((name, first, lane, count, length))
    widths = {"qkv": round_up(3 * part_width, LANES), "out": D, "up": SPAN, "down": D}
    padded = {"qkv": D, "out": round_up(part_width, LANES), "up": D, "down": SPAN}
    tail_first = items["tail"][0] // LANES
    scratch = [pltpu.VMEM((total + 2 * MARGIN, LANES), f32), pltpu.SemaphoreType.DMA((len(work),))]
    for name, begin, count in work:
        scratch.append(pltpu.VMEM((round_up(count, BLOCK), widths[name]), bf16))
    up_rows = [count for name, _, count in work if name == "up"]
    if up_rows:
        scratch.append(pltpu.VMEM((SPAN // LANES, up_rows[0], LANES), f32))
    units = BLOCK // phase_count(items["qkv"][2])
    qkv_tiles = widths["qkv"] // LANES
    has_qkv = any(name == "qkv" for name, _, _ in work)
    if has_qkv:
        scratch.append(pltpu.VMEM((qkv_tiles, BLOCK, LANES), f32))
    split = place is not None
    shard_rows = total // 2
    half_a = round_up(shard_rows // 2, 16)
    half_b = round_up(shard_rows - half_a, 16)
    if split:
        scratch += [
            pltpu.VMEM((2, half_a, LANES), bf16),
            pltpu.VMEM((2, half_b, LANES), bf16),
            pltpu.SemaphoreType.DMA((4,)),
        ]

    def kernel(*refs):
        refs = list(refs)
        place_ref = refs.pop(0) if split else None
        mats = {name: refs.pop(0) for name, _, _ in work}
        vecs = {entry[0]: refs.pop(0) for entry in vec_work}
        outs = [refs.pop(0) for _ in range(4 if split else 1)]
        flat = refs.pop(0)
        sems = refs.pop(0)
        bufs = {name: refs.pop(0) for name, _, _ in work}
        tall = refs.pop(0) if up_rows else None
        tmp = refs.pop(0) if has_qkv else None
        region = pl.program_id(0)
        copies = {}
        for index, (name, begin, count) in enumerate(work):
            rows_read = round_up(count, BLOCK)
            if name in ("qkv", "up"):
                at = pl.multiple_of(region * widths[name], LANES)
                source = mats[name].at[pl.ds(begin, rows_read), pl.ds(at, widths[name])]
            else:
                at = pl.multiple_of(region * padded[name] + begin, BLOCK)
                source = mats[name].at[pl.ds(at, rows_read), :]
            copies[name] = pltpu.make_async_copy(source, bufs[name], sems.at[index])
            copies[name].start()
        if high_row > tail_first:
            clear = high_row - tail_first
            flat[pl.ds(tail_first + base, clear), :] = jnp.zeros((clear, LANES), f32)

        def merge(rows, value, keep):
            flat[rows, :] = jnp.where(keep, value, flat[rows, :])

        def lay_row(tile_of, first, lane_at, width, count, stride):
            tiles = -(-width // LANES)
            lane = lax.broadcasted_iota(jnp.int32, (count, LANES), 1)
            end = lane_at + width - (tiles - 1) * LANES
            before = None
            for tile in range(tiles):
                now = tile_of(tile)
                if lane_at == 0:
                    value = now
                else:
                    value = now if before is None else jnp.where(lane < LANES - lane_at, now, before)
                    value = pltpu.roll(value, lane_at, 1)
                rows = pl.ds(first + tile, count, stride=stride)
                if tile == 0 and lane_at > 0:
                    merge(rows, value, lane >= lane_at)
                elif tile == tiles - 1 and end < LANES:
                    merge(rows, value, lane < end)
                else:
                    flat[rows, :] = value
                before = now
            if end > LANES:
                rows = pl.ds(first + tiles, count, stride=stride)
                merge(rows, pltpu.roll(before, lane_at, 1), lane < end - LANES)

        for name, begin, count in work:
            start, _, width = items[name]
            phases = phase_count(width)
            stride = width * phases // LANES
            buf = bufs[name]
            copies[name].wait()
            if name in ("out", "down"):
                first, lane_at, _ = lane_rows(start + begin * width, 1)

                def lay_block(at, rows_now, buf=buf, first=first, lane_at=lane_at, width=width, stride=stride):
                    source = pl.ds(pl.multiple_of(at, BLOCK), rows_now)
                    lay_row(
                        lambda tile: buf[source, tile * LANES : (tile + 1) * LANES].astype(f32),
                        first + base + stride * at,
                        lane_at,
                        width,
                        rows_now,
                        stride,
                    )

                def step_of(step, carry, lay_block=lay_block):
                    lay_block(step * BLOCK, BLOCK)
                    return carry

                lax.fori_loop(0, count // BLOCK, step_of, 0)
                if count % BLOCK:
                    lay_block(count // BLOCK * BLOCK, count % BLOCK)
            elif name == "qkv":

                def qkv_step(step, carry, buf=buf, start=start, begin=begin, width=width, phases=phases, stride=stride):
                    source = pl.ds(pl.multiple_of(step * BLOCK, BLOCK), BLOCK)
                    for tile in range(qkv_tiles):
                        tmp[tile] = buf[source, tile * LANES : (tile + 1) * LANES].astype(f32)
                    for phase in range(phases):
                        first, lane_at, _ = lane_rows(start + (begin + phase) * width, 1)
                        lay_row(
                            lambda tile, phase=phase: tmp[tile, pl.ds(phase, units, stride=phases), :],
                            first + base + stride * units * step,
                            lane_at,
                            width,
                            units,
                            stride,
                        )
                    return carry

                lax.fori_loop(0, count // BLOCK, qkv_step, 0)
            else:
                number = count // phases
                tiles = -(-width // LANES)
                for tile in range(tiles):
                    tall[tile] = buf[:, tile * LANES : (tile + 1) * LANES].astype(f32)
                spots = []
                for phase in range(phases):
                    first, lane_at, _ = lane_rows(start + (begin + phase) * width, 1)
                    spots.append((first + base, lane_at))
                lane = lax.broadcasted_iota(jnp.int32, (number, LANES), 1)

                def up_step(tile, carry, spots=spots, lane=lane, number=number, phases=phases, stride=stride):
                    for phase, (first, lane_at) in enumerate(spots):
                        picks = pl.ds(phase, number, stride=phases)
                        value = tall[tile, picks, :]
                        if lane_at > 0:
                            value = pltpu.roll(
                                jnp.where(lane < LANES - lane_at, value, tall[tile - 1, picks, :]), lane_at, 1
                            )
                        flat[pl.ds(first + tile, number, stride=stride), :] = value
                    return carry

                lax.fori_loop(1, tiles - 1, up_step, 0)
                for phase, (first, lane_at) in enumerate(spots):
                    picks = pl.ds(phase, number, stride=phases)
                    rows = pl.ds(first, number, stride=stride)
                    value = tall[0, picks, :]
                    if lane_at > 0:
                        merge(rows, pltpu.roll(value, lane_at, 1), lane >= lane_at)
                    else:
                        flat[rows, :] = value
                    end = lane_at + width - (tiles - 1) * LANES
                    last = tall[tiles - 1, picks, :]
                    value = last
                    if lane_at > 0:
                        value = pltpu.roll(
                            jnp.where(lane < LANES - lane_at, last, tall[tiles - 2, picks, :]), lane_at, 1
                        )
                    merge(pl.ds(first + tiles - 1, number, stride=stride), value, lane < end)
                    if end > LANES:
                        merge(
                            pl.ds(first + tiles, number, stride=stride),
                            pltpu.roll(last, lane_at, 1),
                            lane < end - LANES,
                        )
        for name, first, lane_at, count, length in vec_work:
            shape = (count, LANES)
            position = lax.broadcasted_iota(jnp.int32, shape, 0) * LANES + lax.broadcasted_iota(jnp.int32, shape, 1)
            keep = (position >= lane_at) & (position < lane_at + length)
            merge(pl.ds(first + base, count), vecs[name][0, pl.ds(0, count), :], keep)

        def narrow(target, origin, count):
            chunk = 64

            def step_of(step, carry):
                target(pl.ds(pl.multiple_of(step * chunk, chunk), chunk), flat[pl.ds(origin + step * chunk, chunk), :])
                return carry

            lax.fori_loop(0, count // chunk, step_of, 0)
            left = count % chunk
            if left:
                done = count // chunk * chunk
                target(pl.ds(done, left), flat[pl.ds(origin + done, left), :])

        if not split:

            def put(rows, value):
                outs[0][0, rows, :] = value.astype(bf16)

            narrow(put, MARGIN, total)
            return
        stage_a, stage_b, out_sems = refs
        keep_a, send_a, keep_b, send_b = outs
        far_x = jnp.bitwise_xor(region, place_ref[0])
        for part in range(2):

            def put_a(rows, value, part=part):
                stage_a[part, rows, :] = value.astype(bf16)

            def put_b(rows, value, part=part):
                stage_b[part, rows, :] = value.astype(bf16)

            narrow(put_a, MARGIN + part * shard_rows, half_a)
            narrow(put_b, MARGIN + part * shard_rows + half_a, half_b)
            far_y = jnp.bitwise_xor(part, place_ref[1])
            for far in range(2):

                @pl.when(far_x == far)
                def _(far=far, part=part, far_y=far_y):
                    pltpu.make_async_copy(
                        stage_a.at[part], (keep_a, send_a)[far].at[far_y], out_sems.at[2 * part]
                    ).start()

                @pl.when(far_y == far)
                def _(far=far, part=part):
                    pltpu.make_async_copy(
                        stage_b.at[part], (keep_b, send_b)[far].at[far_x], out_sems.at[2 * part + 1]
                    ).start()

        for part in range(2):
            pltpu.make_async_copy(stage_a.at[part], keep_a.at[0], out_sems.at[2 * part]).wait()
            pltpu.make_async_copy(stage_b.at[part], keep_b.at[0], out_sems.at[2 * part + 1]).wait()

    any_spec = pl.BlockSpec(memory_space=pl.ANY)
    in_specs = [any_spec for _ in work]
    args = [grads[name] for name, _, _ in work]
    for name, first, lane, count, length in vec_work:
        padded_vec = jnp.pad(vectors[name], ((0, 0), (lane, round_up(count, 8) * LANES - lane - length)))
        args.append(padded_vec.reshape(2, -1, LANES))
        in_specs.append(pl.BlockSpec((1, round_up(count, 8), LANES), lambda r, *_: (r, 0, 0)))
    if split:
        shape_a = jax.ShapeDtypeStruct((2, half_a, LANES), bf16)
        shape_b = jax.ShapeDtypeStruct((2, half_b, LANES), bf16)
        out_shape = [shape_a, shape_a, shape_b, shape_b]
        out_specs = [any_spec] * 4
        args = [place] + args
    else:
        out_shape = [jax.ShapeDtypeStruct((2, total, LANES), bf16)]
        out_specs = [pl.BlockSpec((1, total, LANES), lambda r, *_: (r, 0, 0))]
    return pl.pallas_call(
        kernel,
        grid_spec=pltpu.PrefetchScalarGridSpec(
            num_scalar_prefetch=1 if split else 0,
            grid=(2,),
            in_specs=in_specs,
            out_specs=out_specs,
            scratch_shapes=scratch,
        ),
        out_shape=out_shape,
        compiler_params=pltpu.CompilerParams(vmem_limit_bytes=60 * 1024 * 1024),
        name="pack_range_%d" % low_row,
    )(*args)


def attention_forward(joined, seq_len, heads, group_width):
    rows = joined.shape[0] // 2
    width = joined.shape[1] // 2
    out_width = round_up(group_width, LANES)
    scale = 1.0 / math.sqrt(HEAD_DIM)

    def kernel(in_ref, mixed_ref, total_ref):
        column = lax.broadcasted_iota(jnp.int32, (1, rows), 1)
        valid = column < seq_len
        mixed_ref[:, group_width:] = jnp.zeros((rows, out_width - group_width), bf16)
        for head in range(heads):
            at = head * HEAD_DIM
            query = in_ref[:, at : at + HEAD_DIM]
            key = in_ref[:, group_width + at : group_width + at + HEAD_DIM]
            value = in_ref[:, 2 * group_width + at : 2 * group_width + at + HEAD_DIM]
            raw = lax.dot_general(query, key, (((1,), (1,)), ((), ())), preferred_element_type=f32) * scale
            raw = jnp.where(valid, raw, -1e30)
            top = jnp.max(raw, -1, keepdims=True)
            weight = jnp.exp(raw - top)
            total = jnp.sum(weight, -1, keepdims=True)
            mixed = jnp.dot(weight.astype(bf16), value, preferred_element_type=f32) / total
            mixed_ref[:, at : at + HEAD_DIM] = mixed.astype(bf16)
            total_ref[:, head : head + 1] = top + jnp.log(total)

    return pl.pallas_call(
        kernel,
        grid=(2, 2),
        in_specs=[pl.BlockSpec((rows, width), lambda i, r: (i, r))],
        out_specs=[
            pl.BlockSpec((rows, out_width), lambda i, r: (i, r)),
            pl.BlockSpec((rows, LANES), lambda i, r: (i, r)),
        ],
        out_shape=[
            jax.ShapeDtypeStruct((2 * rows, 2 * out_width), bf16),
            jax.ShapeDtypeStruct((2 * rows, 2 * LANES), f32),
        ],
        compiler_params=pltpu.CompilerParams(vmem_limit_bytes=60 * 1024 * 1024),
        name="attention_forward",
    )(joined)


def attention_backward(joined, mixed_grad, totals, seq_len, heads, group_width):
    rows = joined.shape[0] // 2
    width = joined.shape[1] // 2
    out_width = round_up(group_width, LANES)
    scale = 1.0 / math.sqrt(HEAD_DIM)

    def kernel(in_ref, grad_ref, total_ref, out_ref):
        key_row = lax.broadcasted_iota(jnp.int32, (rows, 1), 0)
        valid = key_row < seq_len
        total_rows = jnp.transpose(total_ref[...])
        out_ref[:, 3 * group_width :] = jnp.zeros((rows, width - 3 * group_width), bf16)
        for head in range(heads):
            at = head * HEAD_DIM
            query = in_ref[:, at : at + HEAD_DIM]
            key = in_ref[:, group_width + at : group_width + at + HEAD_DIM]
            value = in_ref[:, 2 * group_width + at : 2 * group_width + at + HEAD_DIM]
            grad = grad_ref[:, at : at + HEAD_DIM]
            raw = lax.dot_general(key, query, (((1,), (1,)), ((), ())), preferred_element_type=f32) * scale
            probs = jnp.where(valid, jnp.exp(raw - total_rows[head : head + 1, :]), 0.0)
            value_grad = jnp.dot(probs.astype(bf16), grad, preferred_element_type=f32)
            prob_grad = lax.dot_general(value, grad, (((1,), (1,)), ((), ())), preferred_element_type=f32)
            row_dot = jnp.sum(probs * prob_grad, 0, keepdims=True)
            score_grad = (probs * (prob_grad - row_dot) * scale).astype(bf16)
            key_grad = jnp.dot(score_grad, query, preferred_element_type=f32)
            query_grad = lax.dot_general(score_grad, key, (((0,), (0,)), ((), ())), preferred_element_type=f32)
            out_ref[:, at : at + HEAD_DIM] = query_grad.astype(bf16)
            out_ref[:, group_width + at : group_width + at + HEAD_DIM] = key_grad.astype(bf16)
            out_ref[:, 2 * group_width + at : 2 * group_width + at + HEAD_DIM] = value_grad.astype(bf16)

    return pl.pallas_call(
        kernel,
        grid=(2, 2),
        in_specs=[
            pl.BlockSpec((rows, width), lambda i, r: (i, r)),
            pl.BlockSpec((rows, out_width), lambda i, r: (i, r)),
            pl.BlockSpec((rows, LANES), lambda i, r: (i, r)),
        ],
        out_specs=pl.BlockSpec((rows, width), lambda i, r: (i, r)),
        out_shape=jax.ShapeDtypeStruct(joined.shape, bf16),
        compiler_params=pltpu.CompilerParams(vmem_limit_bytes=60 * 1024 * 1024),
        name="attention_backward",
    )(joined, mixed_grad, totals)


def norm_parts(values):
    center = values - jnp.mean(values, -1, keepdims=True)
    variance = jnp.mean(center * center, -1, keepdims=True)
    scale = lax.rsqrt(variance + norm_eps)
    return center * scale, scale


def norm_back(grad, unit, scale, gain):
    scaled = grad * gain
    return scale * (
        scaled - jnp.mean(scaled, -1, keepdims=True) - unit * jnp.mean(scaled * unit, -1, keepdims=True)
    )


def gelu_tanh(values):
    return jax.nn.gelu(values, approximate=True)


def mul(left, right):
    return jnp.dot(left, right, preferred_element_type=f32)


def mul_wt(left, right):
    return lax.dot_general(left, right, (((1,), (1,)), ((), ())), preferred_element_type=f32)


def mul_tw(left, right):
    return lax.dot_general(left, right, (((0,), (0,)), ((), ())), preferred_element_type=f32)


def reduce_shards(grads, vectors, group_count, wide_count, shard_rows):
    region_rows = wide_count * shard_rows
    if wide_count != 8:
        (packed,) = pack_range(grads, vectors, 0, region_rows, group_count)
        groups = [
            [dp * group_count + 2 * half + core for dp in range(wide_count) for half in range(group_count // 2)]
            for core in range(2)
        ]
        packed = packed.reshape(2, wide_count, shard_rows, LANES).transpose(1, 0, 2, 3)
        return lax.psum_scatter(
            packed.reshape(-1, LANES), BOTH, scatter_dimension=0, axis_index_groups=groups, tiled=True
        ).astype(f32)
    x_pos = lax.axis_index("group") // 2
    y_pos = lax.axis_index("dp") % 2
    z_pos = lax.axis_index("dp") // 2
    place = jnp.stack([x_pos, y_pos]).astype(jnp.int32)
    x_pairs = [(one, one ^ 2) for one in range(group_count)]
    y_pairs = [(one, one ^ 1) for one in range(wide_count)]
    total = None
    for plane in (3, 2, 1, 0):
        keep_a, send_a, keep_b, send_b = pack_range(
            grads, vectors, 2 * plane * shard_rows, 2 * (plane + 1) * shard_rows, group_count, place
        )
        got_a = lax.ppermute(send_a, "group", x_pairs)
        got_b = lax.ppermute(send_b, "dp", y_pairs)
        next_a = (keep_a[1].astype(f32) + got_a[1].astype(f32)).astype(bf16)
        next_b = (keep_b[1].astype(f32) + got_b[1].astype(f32)).astype(bf16)
        back_a = lax.ppermute(next_a, "dp", y_pairs)
        back_b = lax.ppermute(next_b, "group", x_pairs)
        sum_a = (keep_a[0].astype(f32) + got_a[0].astype(f32) + back_a.astype(f32)).astype(bf16)
        sum_b = (keep_b[0].astype(f32) + got_b[0].astype(f32) + back_b.astype(f32)).astype(bf16)
        payload = jnp.concatenate([sum_a, sum_b])
        mine = jnp.where(z_pos == plane, payload.astype(f32), 0.0)
        total = mine if total is None else total + mine
        for other in range(4):
            if other != plane:
                pairs = [(2 * other + y, 2 * plane + y) for y in range(2)]
                total = total + lax.ppermute(payload, "dp", pairs).astype(f32)
    return total[:shard_rows]


def local(images, cotangent, flags, master, first_moment, second_moment):
    group_count = lax.axis_size("group")
    wide_count = lax.axis_size("dp")
    part_width = D // group_count
    part_hidden = FF // group_count
    shard = master.shape[0]
    shard_rows = shard // LANES
    heads = HEADS // group_count
    core = lax.axis_index("group") % 2
    pair = [(one, one ^ 1) for one in range(group_count)]

    def swap(values):
        return lax.ppermute(values, "group", pair)

    items = region_items(group_count)
    places, _ = vector_rows(items)
    shard_low = master.reshape(shard_rows, LANES).astype(bf16)
    groups = [
        [dp * group_count + 2 * half + one for dp in range(wide_count) for half in range(group_count // 2)]
        for one in range(2)
    ]
    gathered = lax.all_gather(shard_low, BOTH, axis=0, tiled=False, axis_index_groups=groups)
    pieces = gathered.reshape(wide_count, group_count // 2, shard_rows, LANES)

    seq_len = images.shape[1]
    rows = round_up(seq_len, 16)
    flag_val = flags[0].astype(f32)
    pad_rows = ((0, rows - seq_len), (0, 0))
    own_in = jnp.concatenate(
        [jnp.pad(images[0], pad_rows), jnp.pad((cotangent[0].astype(f32) * flag_val).astype(bf16), pad_rows)]
    )
    other_in = swap(own_in)
    tokens = jnp.concatenate([own_in[:rows], other_in[:rows]]).astype(f32)
    branch_grad = jnp.concatenate([own_in[rows:], other_in[rows:]])
    out_grad = branch_grad.astype(f32)

    w_qkv, w_out, w_up, w_down, vecs = unpack_regions(pieces, group_count)

    def vector(name):
        at, _, lane, count, length = places[name]
        return vecs[:, at : at + count].reshape(2, count * LANES)[:, lane : lane + length]

    at, _, lane, count, length = places["tail"]
    tail_rows = vecs[0, at : at + count]
    tail_rows = jnp.where(core == 0, tail_rows, swap(tail_rows))
    shared = tail_rows.reshape(-1)[lane : lane + length].reshape(6, D)
    qv = vector("qv")
    blank = jnp.zeros((2, part_width), f32)
    bias_full = jnp.concatenate(
        [qv[:, :part_width], blank, qv[:, part_width:], jnp.zeros((2, w_qkv.shape[1] // 2 - 3 * part_width), f32)], 1
    ).reshape(-1)
    up_bias = jnp.pad(vector("upb"), ((0, 0), (0, SPAN - part_hidden))).reshape(-1)

    unit_one, scale_one = norm_parts(tokens)
    normed = (unit_one * shared[0] + shared[1]).astype(bf16)
    joined = (mul(normed, w_qkv) + bias_full).astype(bf16)
    mixed, totals = attention_forward(joined, seq_len, heads, part_width)
    proj = mul(mixed, w_out)
    proj_other = swap(proj.astype(bf16)).astype(f32)
    proj_other = jnp.concatenate([proj_other[rows:], proj_other[:rows]])
    hidden_state = tokens + (proj + proj_other) + shared[2]
    unit_two, scale_two = norm_parts(hidden_state)
    normed_two = (unit_two * shared[3] + shared[4]).astype(bf16)
    pre_act = mul(normed_two, w_up) + up_bias
    activ, gelu_back = jax.vjp(gelu_tanh, pre_act)
    activ = activ.astype(bf16)
    branch = mul(activ, w_down)
    branch_other = swap(branch[rows:].astype(bf16)).astype(f32)
    output = flag_val * (hidden_state[:seq_len] + (branch[:seq_len] + branch_other[:seq_len] + shared[5]))
    output = output.astype(bf16)

    activ_grad = mul_wt(branch_grad, w_down)
    pre_grad = gelu_back(activ_grad)[0].astype(bf16)
    normed_two_part = mul_wt(pre_grad, w_up)
    part_other = swap(normed_two_part.astype(bf16)).astype(f32)
    normed_two_grad = normed_two_part + jnp.concatenate([part_other[rows:], part_other[:rows]])
    hidden_grad = out_grad + norm_back(normed_two_grad, unit_two, scale_two, shared[3])
    proj_grad = hidden_grad.astype(bf16)
    mixed_grad = mul_wt(proj_grad, w_out).astype(bf16)
    joined_grad = attention_backward(joined, mixed_grad, totals, seq_len, heads, part_width)
    normed_part = mul_wt(joined_grad, w_qkv)
    normed_own = normed_part[:rows] + swap(normed_part[rows:].astype(bf16)).astype(f32)
    token_grad = hidden_grad[:rows] + norm_back(normed_own, unit_one[:rows], scale_one[:rows], shared[0])
    token_grad = token_grad[:seq_len].astype(bf16)

    shared_grad = jnp.stack(
        [
            jnp.sum(normed_own * unit_one[:rows], 0),
            jnp.sum(normed_own, 0),
            jnp.sum(proj_grad[:rows].astype(f32), 0),
            jnp.sum(normed_two_grad[:rows] * unit_two[:rows], 0),
            jnp.sum(normed_two_grad[:rows], 0),
            jnp.sum(branch_grad[:rows].astype(f32), 0),
        ]
    )
    shared_sum = lax.psum(shared_grad, BOTH).reshape(-1)

    grads = {
        "down": mul_tw(activ, branch_grad).astype(bf16),
        "up": mul_tw(normed_two, pre_grad).astype(bf16),
        "out": mul_tw(mixed, proj_grad).astype(bf16),
        "qkv": mul_tw(normed, joined_grad).astype(bf16),
    }
    joined_sums = jnp.sum(joined_grad.astype(f32), 0).reshape(2, -1)
    vectors = {
        "qv": jnp.concatenate(
            [joined_sums[:, :part_width], joined_sums[:, 2 * part_width : 3 * part_width]], 1
        ),
        "upb": jnp.sum(pre_grad.astype(f32), 0).reshape(2, -1)[:, :part_hidden],
    }
    grad_rows = reduce_shards(grads, vectors, group_count, wide_count, shard_rows)

    tail_start = items["tail"][0]
    owner = tail_start // shard
    inside = tail_start - owner * shard
    is_owner = (lax.axis_index("dp") == owner) & (lax.axis_index("group") == 0)
    tail_flat = jnp.pad(jnp.where(is_owner, shared_sum, 0.0), (inside, shard - inside - 6 * D))
    grad_sum = grad_rows + tail_flat.reshape(shard_rows, LANES)

    first_rows = first_moment.reshape(shard_rows, LANES)
    second_rows = second_moment.reshape(shard_rows, LANES)
    new_first = beta_one * first_rows + (1.0 - beta_one) * grad_sum
    new_second = beta_two * second_rows + (1.0 - beta_two) * grad_sum * grad_sum
    corrected = new_first / (1.0 - beta_one**adam_step)
    var_hat = new_second / (1.0 - beta_two**adam_step)
    new_master = master.reshape(shard_rows, LANES) - learn_rate * corrected / (jnp.sqrt(var_hat) + adam_eps)
    return (
        output[None],
        token_grad[None],
        grad_sum.reshape(-1),
        new_master.reshape(-1),
        new_first.reshape(-1),
        new_second.reshape(-1),
    )


def solution(mesh):
    whole = P(BOTH, None, None)
    flat = P(BOTH)
    return jax.shard_map(
        local,
        mesh=mesh,
        in_specs=(whole, whole, flat, flat, flat, flat),
        out_specs=(whole, whole, flat, flat, flat, flat),
        check_vma=False,
    )
```
